32 devices in a mesh: group: 2 (over x), seq: 16 (over z, y, core).
Axes of the slice: x: 2, y: 2, z: 4, core: 2. Of those that a mesh axis runs over, the one named last changes fastest.
Arguments:
- resid_in: bfloat16 [512, 2880], P(('group', 'seq')), parts along dimension 0, may hold values from -6 to 6
- queries: bfloat16 [512, 4096], P('group'), parts along dimension 0, may hold values from -256 to 256
- key_cache: bfloat16 [8, 8192, 512], P('group', 'seq'), parts along dimension 0, may hold values from -6 to 6
- value_cache: bfloat16 [8, 8192, 512], P('group', 'seq'), parts along dimension 0, may hold values from -6 to 6
- lengths: int32 [8], P('group'), parts along dimension 0, may hold values from 8 to 8128, as said below
- expert_ids: int32 [512, 4], P(('group', 'seq')), parts along dimension 0, may hold values from 0 to 15, all different within a row; in each aligned block of 16 rows (0 to 15, 16 to 31, ...) at most 8 rows name the same one
- expert_weights: float32 [512, 4], P(('group', 'seq')), parts along dimension 0, may hold values from 0.1 to 0.6
- out_proj: bfloat16 [4096, 2880], P('seq'), may hold values from -0.09375 to 0.09375
- gate_proj: bfloat16 [2880, 23040], P(None, 'seq'), may hold values from -0.109375 to 0.109375
- up_proj: bfloat16 [2880, 23040], P(None, 'seq'), may hold values from -0.109375 to 0.109375
- down_proj: bfloat16 [23040, 2880], P('seq'), may hold values from -0.15625 to 0.15625
- moe_gain: float32 [2880], replicated, may hold values from 0.5 to 2
- attn_gain: float32 [2880], replicated, may hold values from 0.5 to 2
- query_proj: bfloat16 [2880, 4096], P(None, 'seq'), may hold values from -0.109375 to 0.109375
Outputs:
- stream_out: bfloat16 [512, 2880], P(('group', 'seq')), parts along dimension 0
- next_queries: bfloat16 [512, 4096], P('group', 'seq'), parts along dimension 0
The draws below stay inside these ranges and needn't reach their ends.
There are 2 independent parts, one for each index of `group`. The reference program is written for one: setup_inputs(seed, part) draws one part's arguments, and reference() takes and returns one part's arrays. A program takes and returns all parts, laid end to end along the dimension named above; an argument that names none is the same for every part. Nothing has to cross between parts.
Inputs may be any that keep to these rules, and one draw needn't show every extreme that they name: `expert_ids`: in each aligned block of 16 rows (the rows of one device) no expert is named by more than 8 rows, a bound that some block reaches. `lengths`: some request has exactly 8128 cached positions.
All inputs are finite; a program needn't handle non-finite values.
Results may differ from the reference program's by a relative error of at most 0.012.
Values may be sent and summed in bfloat16 or wider, within the bound.
A program may use at most 128 MiB of HBM per device.

```python
import math
import jax
import jax.numpy as jnp
import numpy as np
from jax import lax

D = 2880
H = 64
KVH = 8
HEAD_SIZE = 64
EXPERTS = 16
FF = 1440
TOPK = 4
REQS = 4
QROWS = 64
SEQ_DEV = 512
ROWS = 256
CACHE = 8192
TOK_DEV = 16
CAP = 8
N_SEQ = 16


def shared_keys(key):
    drawn = jax.random.normal(jax.random.fold_in(key, 11), (REQS, CACHE, KVH * HEAD_SIZE), jnp.float32)
    return jnp.clip(drawn, -6.0, 6.0)


def draw_key_cache(key, part):
    keys_all = shared_keys(key)
    return keys_all.astype(jnp.bfloat16)


def draw_queries(key, part):
    normal_part = jnp.clip(jax.random.normal(jax.random.fold_in(key, 13), (ROWS, H * HEAD_SIZE), jnp.float32), -4.0, 4.0) * 3.0
    return normal_part.astype(jnp.bfloat16)


def draw_lengths(key, part):
    top_length = CACHE - QROWS
    drawn = jax.random.randint(jax.random.fold_in(key, 17), (REQS,), 8, top_length + 1)
    chosen = jax.random.randint(jax.random.fold_in(key, 19), (), 0, REQS)
    return jnp.where(jnp.arange(REQS) == chosen, top_length, drawn).astype(jnp.int32)


def shard_levels(own_key, shape, cuts, least, high):
    def one(dim, parts):
        steps = jax.random.uniform(jax.random.fold_in(jax.random.fold_in(own_key, 6), dim), (parts,), jnp.float32, least / len(cuts), high / len(cuts))
        return jnp.repeat(jnp.exp(steps), shape[dim] // parts).reshape((-1,) + (1,) * (len(shape) - dim - 1))

    factor_of = one(*cuts[0])
    for cut in cuts[1:]:
        factor_of = factor_of * one(*cut)
    return factor_of


def deal_out(rng, own, number, rows, amount, top, most, slope):
    order = jax.random.permutation(rng, amount)
    crowded, usual = portions_of(amount, rows * top, most, slope, True), portions_of(amount, rows * top, most, slope, False)
    places = jnp.arange(amount)

    def named(sizes, offset_by):
        used = int((sizes > 0).sum())
        fixed = max(1, used // 4)
        passed = fixed + (places - fixed + offset_by * (used - fixed)) % max(1, amount - fixed)
        return jnp.zeros((amount,), jnp.int32).at[order[jnp.where(places < fixed, places, passed)]].set(jnp.asarray(sizes, jnp.int32))

    sizes = jnp.where(number % 4 == 0, named(crowded, number // 4), named(usual, number - number // 4 - 1))
    mixed = jax.random.permutation(jax.random.fold_in(own, 3), amount)
    donor, sink = mixed[0:amount // 2 * 2:2], mixed[1:amount // 2 * 2:2]
    margin = jnp.minimum(sizes[donor] - 1, most - sizes[sink]) // 2
    margin = jnp.where((donor == order[0]) | (sink == order[0]) | (sizes[sink] == 0), 0, jnp.maximum(margin, 0))
    passed = jax.random.randint(jax.random.fold_in(own, 4), (amount // 2,), 0, 1 << 20) % (margin + 1)
    sizes = sizes.at[donor].add(-passed).at[sink].add(passed)
    members = jnp.searchsorted(jnp.cumsum(sizes), jnp.arange(rows * top), side="right").astype(jnp.int32)
    table = members.reshape(top, rows).T
    table = table[jax.random.permutation(jax.random.fold_in(own, 1), rows)]
    offset_by = jax.random.randint(jax.random.fold_in(own, 2), (rows, 1), 0, top)
    return jnp.take_along_axis(table, (jnp.arange(top)[None, :] + offset_by) % top, axis=1)


def portions_of(amount, total, reach, slope, full):
    loads = [(1 << 20) // math.isqrt(rank ** slope) + 1 for rank in range(1, amount + 1)]
    largest = reach if full else min(reach, max(-(-total // amount), total * loads[0] // sum(loads)))
    least = 1 if total - largest >= amount - 1 else 0
    given, surplus = [largest] + [least] * (amount - 1), total - largest - least * (amount - 1)
    while surplus > 0:
        movable = [i for i in range(1, amount) if given[i] < largest] or [i for i in range(1, amount) if given[i] < reach]
        whole, budget = sum([loads[i] for i in movable]), surplus
        for i in movable:
            addition = min(reach - given[i], max(1, budget * loads[i] // whole), surplus)
            given[i] = given[i] + addition
            surplus = surplus - addition
    return np.array(given)


def noise(rng, extent, width, most, cuts=(), kind=jnp.bfloat16):
    gain = shard_levels(rng, extent, cuts, -0.22, 0.18) if cuts else 1.0
    result = jax.random.normal(rng, extent, jnp.float32) * width * gain
    return jnp.minimum(jnp.maximum(result, -most), most).astype(kind)


def setup_inputs(seed: int = 0, part: int = 0) -> dict:
    keys = jax.random.split(jax.random.key(seed), 15)
    part_keys = jax.random.split(jax.random.fold_in(keys[14], part), 15)
    resid_in = noise(part_keys[0], (ROWS, D), 1.0, 6.0, ((0, 16),))
    queries = draw_queries(jax.random.fold_in(jax.random.fold_in(keys[14], part), 71), part)
    key_cache = draw_key_cache(jax.random.fold_in(jax.random.fold_in(keys[14], part), 71), part)
    value_cache = noise(part_keys[3], (REQS, CACHE, KVH * HEAD_SIZE), 1.0, 6.0, ((1, 16),))
    lengths = draw_lengths(jax.random.fold_in(jax.random.fold_in(keys[14], part), 71), part)
    expert_ids_keys = jax.random.split(jax.random.fold_in(part_keys[5], 1), ROWS // TOK_DEV)
    expert_ids_turns = jax.random.permutation(jax.random.fold_in(part_keys[5], 3), ROWS // TOK_DEV)
    expert_ids = jax.vmap(lambda own, number: deal_out(jax.random.fold_in(part_keys[5], 2), own, number, TOK_DEV, EXPERTS, TOPK, CAP, 2))(expert_ids_keys, expert_ids_turns).reshape((ROWS, TOPK))
    expert_weights = jnp.clip(0.1 + 0.5 * jax.random.uniform(part_keys[6], (ROWS, TOPK), jnp.float32) ** shard_levels(part_keys[6], (ROWS, TOPK), ((0, 16),), -0.2, 0.2), 0.1, 0.6)
    out_proj = noise(keys[7], (H * HEAD_SIZE, D), (H * HEAD_SIZE) ** -0.5, 0.09375, ((0, 16),))
    gate_proj = noise(keys[8], (D, EXPERTS * FF), D ** -0.5, 0.109375, ((1, 16),))
    up_proj = noise(keys[9], (D, EXPERTS * FF), D ** -0.5, 0.109375, ((1, 16),))
    down_proj = noise(keys[10], (EXPERTS * FF, D), FF ** -0.5, 0.15625, ((0, 16),))
    moe_gain = jnp.clip(jnp.exp(jax.random.uniform(keys[11], (D,), jnp.float32, math.log(0.5), math.log(2.0))), 0.5, 2.0)
    attn_gain = jnp.clip(jnp.exp(jax.random.uniform(keys[12], (D,), jnp.float32, math.log(0.5), math.log(2.0))), 0.5, 2.0)
    query_proj = noise(keys[13], (D, H * HEAD_SIZE), D ** -0.5, 0.109375, ((1, 16),))
    return dict(resid_in=resid_in, queries=queries, key_cache=key_cache, value_cache=value_cache, lengths=lengths, expert_ids=expert_ids, expert_weights=expert_weights, out_proj=out_proj, gate_proj=gate_proj, up_proj=up_proj, down_proj=down_proj, moe_gain=moe_gain, attn_gain=attn_gain, query_proj=query_proj)


NEG_FILL = -1e+30

def rms_norm(values, gain_vec):
    wide_vals = values.astype(jnp.float32)
    scaled = wide_vals * lax.rsqrt(lax.optimization_barrier(jnp.mean(wide_vals * wide_vals, axis=-1, keepdims=True)) + 1e-05)
    return (scaled * gain_vec).astype(jnp.bfloat16)

def attention(queries, key_cache, value_cache, lengths):
    groups = H // KVH
    query_grid = queries.reshape(REQS, QROWS, KVH, groups, HEAD_SIZE).transpose(0, 2, 1, 3, 4).reshape(REQS * KVH, QROWS, groups, HEAD_SIZE)
    key_grid = key_cache.reshape(REQS, N_SEQ, SEQ_DEV, KVH, HEAD_SIZE).transpose(0, 3, 1, 2, 4).reshape(REQS * KVH, N_SEQ, SEQ_DEV, HEAD_SIZE)
    value_grid = value_cache.reshape(REQS, N_SEQ, SEQ_DEV, KVH, HEAD_SIZE).transpose(0, 3, 1, 2, 4).reshape(REQS * KVH, N_SEQ, SEQ_DEV, HEAD_SIZE)
    limits = jnp.repeat(lengths, KVH)
    position = jnp.arange(N_SEQ, dtype=jnp.int32)[:, None] * SEQ_DEV + jnp.arange(SEQ_DEV, dtype=jnp.int32)[None, :]

    def one_head(operands):
        head_queries, head_keys, head_values, limit = operands
        score_matrix = jnp.einsum('xln,rhn->rxlh', head_queries.astype(jnp.float32), head_keys.astype(jnp.float32)) * HEAD_SIZE ** (-0.5)
        allowed = position[:, None, None, :] <= limit + jnp.arange(QROWS, dtype=jnp.int32)[None, :, None, None]
        masked = jnp.where(allowed, score_matrix, NEG_FILL)
        maxima = lax.optimization_barrier(jnp.max(masked, axis=-1))
        chances = jnp.where(allowed, jnp.exp(masked - maxima[..., None]), 0.0)
        totals = lax.optimization_barrier(jnp.sum(chances, axis=-1))
        rounded_values = lax.optimization_barrier(chances.astype(jnp.bfloat16)).astype(jnp.float32)
        running_totals = jnp.einsum('ysan,ynv->ysav', rounded_values, head_values.astype(jnp.float32))
        largest = lax.optimization_barrier(jnp.max(maxima, axis=0))
        factor = jnp.exp(maxima - largest[None])
        numer = lax.optimization_barrier(jnp.sum(running_totals * factor[..., None], axis=0))
        denom = lax.optimization_barrier(jnp.sum(totals * factor, axis=0))
        return (numer / denom[..., None]).astype(jnp.bfloat16)
    attended = lax.map(one_head, (query_grid, key_grid, value_grid, limits))
    return attended.reshape(REQS, KVH, QROWS, groups, HEAD_SIZE).transpose(0, 2, 1, 3, 4).reshape(REQS * QROWS, H * HEAD_SIZE)

def reference(resid_in, queries, key_cache, value_cache, lengths, expert_ids, expert_weights, out_proj, gate_proj, up_proj, down_proj, moe_gain, attn_gain, query_proj):
    attended = attention(queries, key_cache, value_cache, lengths)
    projected = jnp.dot(attended, out_proj, preferred_element_type=jnp.float32)
    hidden_in = (resid_in.astype(jnp.float32) + projected).astype(jnp.bfloat16)
    normed = rms_norm(hidden_in, moe_gain)
    shards = N_SEQ // EXPERTS
    piece_width = FF // shards
    expert_range = jnp.arange(EXPERTS, dtype=jnp.int32)
    picked = lax.optimization_barrier(jnp.sum(expert_weights[:, :, None] * (expert_ids[:, :, None] == expert_range[None, None, :]).astype(jnp.float32), axis=1))

    def one_expert(running, expert_index):
        gate_cols = lax.dynamic_slice_in_dim(gate_proj, expert_index * FF, FF, 1)
        up_cols = lax.dynamic_slice_in_dim(up_proj, expert_index * FF, FF, 1)
        down_rows = lax.dynamic_slice_in_dim(down_proj, expert_index * FF, FF, 0)
        gate_vals = jnp.dot(normed, gate_cols, preferred_element_type=jnp.float32)
        up_vals = jnp.dot(normed, up_cols, preferred_element_type=jnp.float32)
        active = ((up_vals + 1.0) * gate_vals * jax.nn.sigmoid(1.702 * gate_vals)).astype(jnp.bfloat16)
        blocks = jnp.einsum('rsf,sfd->srd', active.reshape(ROWS, shards, piece_width).astype(jnp.float32), down_rows.reshape(shards, piece_width, D).astype(jnp.float32))
        rounded_values = lax.optimization_barrier(blocks.astype(jnp.bfloat16)).astype(jnp.float32)
        output = lax.optimization_barrier(jnp.sum(rounded_values, axis=0))
        weight_col = lax.dynamic_slice_in_dim(picked, expert_index, 1, 1)
        return (running + weight_col * output, None)
    moe_out, unused = lax.scan(one_expert, jnp.zeros((ROWS, D), jnp.float32), expert_range)
    stream_out = (hidden_in.astype(jnp.float32) + moe_out).astype(jnp.bfloat16)
    normed_next = rms_norm(stream_out, attn_gain)
    next_queries = jnp.dot(normed_next, query_proj, preferred_element_type=jnp.float32).astype(jnp.bfloat16)
    return (stream_out, next_queries)
```

```python
import functools
import jax
import jax.numpy as jnp
from jax import lax
from jax.experimental import pallas as pl
from jax.experimental.pallas import tpu as pltpu
from jax.sharding import PartitionSpec as P

H = 64
KVH = 8
HEAD_SIZE = 64
EXPERTS = 16
QROWS = 64
NEG_FILL = -1e30
LOG2E = 1.4426950408889634
PIECES = 4
MESH = pl.DeviceIdType.MESH
STEPS = KVH // 2


def place(i, order):
    out = 0
    for k in order:
        out = out * 2 + (i // 2**k) % 2
    return out


def chunks(total, size, body):
    full = total // size
    if full:

        def step(c, carry):
            body(pl.multiple_of(c * size, size), size)
            return carry

        lax.fori_loop(0, full, step, 0)
    if total % size:
        body(full * size, total % size)


def norm_of(values, gain):
    wide = values.astype(jnp.float32)
    scaled = wide * lax.rsqrt(jnp.mean(wide * wide, axis=-1, keepdims=True) + 1e-05)
    return (scaled * gain).astype(jnp.bfloat16)


def layer_kernel(
    n, orders, cuts, splits,
    len_ref, q_hbm, k_hbm, v_hbm, resid_ref, ids_ref, weights_ref, wo_hbm, gate_hbm, up_hbm,
    down_hbm, wq_hbm, g1_ref, g2_ref,
    stream_ref, nq_ref,
    qb, kb, vb, wo, gate, up, down, wq, accs, mts, acc_ins, mt_ins, parts, part_ins, parts2,
    part2_ins, rows1, rows2, joined, act, att, scores, load_sems, send_sems, recv_sems,
):
    bits = n.bit_length() - 1
    me = lax.axis_index("seq")
    bit = [(me // 2**k) % 2 for k in range(bits)]
    partner = [me + (1 - 2 * bit[k]) * 2**k for k in range(bits)]
    tok, d = resid_ref.shape
    pieces = len(cuts)
    ends = cuts[1:] + (d,)
    per_shard = H // n
    per_piece = per_shard // splits
    requests, span = kb.shape[0], kb.shape[1]
    share = requests // 2
    lanes = share * QROWS
    slots = n // STEPS

    loads = {}

    def load(name, src, dst):
        copy = pltpu.make_async_copy(src, dst, load_sems.at[len(loads)])
        copy.start()
        loads[name] = copy

    for c in range(2):
        rows_c, reqs_c = pl.ds(c * lanes, lanes), pl.ds(c * share, share)
        load(("q", c), q_hbm.at[rows_c], qb.at[rows_c])
        load(("k", c), k_hbm.at[reqs_c], kb.at[reqs_c])
        load(("v", c), v_hbm.at[reqs_c], vb.at[reqs_c])
    load("wo", wo_hbm, wo)
    load("gate", gate_hbm, gate)
    load("up", up_hbm, up)
    load("down", down_hbm, down)
    load("wq", wq_hbm, wq)

    barrier = pltpu.get_barrier_semaphore()
    for k in range(bits):
        pl.semaphore_signal(barrier, inc=1, device_id={"seq": partner[k]}, device_id_type=MESH)

    pairs = H // KVH // 2
    width = pairs * QROWS
    lanes2 = 2 * HEAD_SIZE
    k_lane = lax.broadcasted_iota(jnp.int32, (span, lanes2), 1)
    edge = me * span + lax.broadcasted_iota(jnp.int32, (span, lanes2), 0) - k_lane % QROWS
    q_lane = lax.broadcasted_iota(jnp.int32, (width, lanes2), 1)
    q_row = lax.broadcasted_iota(jnp.int32, (width, lanes2), 0)
    k_low, q_low = k_lane < HEAD_SIZE, q_lane < HEAD_SIZE
    hit = jnp.where(q_lane % QROWS == q_row % QROWS, 1.0, 0.0).astype(jnp.bfloat16)
    ones = jnp.ones((16, span), jnp.bfloat16)
    tile = 128

    def attend(g, c):
        at_g = [place(g * slots, order) for order in orders]
        combos = []
        for r in range(share):
            req = c * share + r
            kv_lanes = pl.ds(pl.multiple_of(g * 128, 128), 128)
            kp = kb[req, :, kv_lanes]
            vt = vb[req, :, kv_lanes].T
            kr = jnp.concatenate([kp[:, HEAD_SIZE:], kp[:, :HEAD_SIZE]], axis=1)
            bar = jnp.where(edge > len_ref[req], NEG_FILL, 0.0).astype(jnp.bfloat16)
            for hh in range(2):
                first = g * 2 * pairs + hh * pairs
                qs = jnp.concatenate(
                    [
                        qb[
                            req * QROWS : (req + 1) * QROWS,
                            pl.ds(pl.multiple_of((first + j) * 128, 128), 128),
                        ]
                        for j in range(pairs)
                    ],
                    axis=0,
                ) * jnp.bfloat16(HEAD_SIZE**-0.5)
                vh = jnp.concatenate([vt[hh * HEAD_SIZE : (hh + 1) * HEAD_SIZE], ones], axis=0)
                for p in range(2):
                    kk = kp if hh == p else kr
                    ka = jnp.where(k_low, bar, kk) if p else jnp.where(k_low, kk, bar)
                    qa = jnp.where(q_low, hit, qs) if p else jnp.where(q_low, qs, hit)
                    combos.append((r, hh, p, ka, qa, vh))

        def score(i):
            ka, qa = combos[i][3:5]
            top = None
            for at in range(0, span, tile):
                s = lax.dot_general(
                    ka[at : at + tile],
                    qa,
                    (((1,), (1,)), ((), ())),
                    preferred_element_type=jnp.float32,
                ) * LOG2E
                scores[i % 2, at : at + tile, :] = s
                here = jnp.max(s.reshape(tile // 8, 8, width), axis=0)
                top = here if top is None else jnp.maximum(top, here)
            return jnp.max(top, axis=0, keepdims=True)

        def weigh(i, m):
            r, hh, p = combos[i][:3]
            vh = combos[i][5]
            base = jnp.maximum(m, NEG_FILL * 0.1)
            acc = None
            for at in range(0, span, tile):
                ch = jnp.exp2((scores[i % 2, at : at + tile, :] - base).astype(jnp.bfloat16))
                one = jnp.dot(vh[:, at : at + tile], ch, preferred_element_type=jnp.float32)
                acc = one if acc is None else acc + one
            t = acc[HEAD_SIZE : HEAD_SIZE + 1]
            acc = acc[:HEAD_SIZE].astype(jnp.bfloat16)
            for j in range(pairs):
                head = hh * (H // KVH) + 2 * j + p
                part, w = divmod(head % per_shard, per_piece)
                part = c * splits + part
                slot = at_g[part % 2] + place(head // per_shard, orders[part % 2])
                src = slice(j * QROWS, (j + 1) * QROWS)
                dst = slice(r * QROWS, (r + 1) * QROWS)
                accs[part][slot, w * HEAD_SIZE : (w + 1) * HEAD_SIZE, dst] = acc[:, src]
                mts[part][slot, w, 0:1, dst] = m[:, src]
                mts[part][slot, w, 1:2, dst] = t[:, src]

        last = None
        for i in range(len(combos) + 1):
            m = score(i) if i < len(combos) else None
            if last is not None:
                weigh(i - 1, last)
            last = m

    def load_wait(*names):
        for name in names:
            loads[name].wait()

    sends = []

    def remote(src, dst, phase, j, k):
        copy = pltpu.make_async_remote_copy(
            src_ref=src,
            dst_ref=dst,
            send_sem=send_sems.at[phase, j],
            recv_sem=recv_sems.at[phase, j],
            device_id={"seq": partner[k]},
            device_id_type=MESH,
        )
        copy.start()
        sends.append(copy)
        return copy

    def land(j):
        return n - 2 * (n >> (j + 1))

    class Halving:
        def __init__(self, c, bufs, inboxes, phases, merge):
            self.order, self.bufs, self.inboxes = orders[c % 2], bufs, inboxes
            self.phases, self.merge, self.flying = phases, merge, {}
            self.keep, self.away, base = [], [], 0
            for j, k in enumerate(self.order):
                half = n >> (j + 1)
                self.away.append(base + (1 - bit[k]) * half)
                base = base + bit[k] * half
                self.keep.append(base)

        def start(self, j):
            half = n >> (j + 1)
            self.flying[j] = [
                remote(
                    buf.at[pl.ds(self.away[j], half)],
                    inbox.at[pl.ds(land(j), half)],
                    phase,
                    j,
                    self.order[j],
                )
                for buf, inbox, phase in zip(self.bufs, self.inboxes, self.phases)
            ]

        def finish(self, j):
            for copy in self.flying[j]:
                copy.wait_recv()
            if j < bits - 1:

                def step(x, carry):
                    self.merge(self.keep[j] + x, land(j) + x, False)
                    return carry

                lax.fori_loop(0, n >> (j + 1), step, 0)
                self.start(j + 1)
            else:
                self.merge(self.keep[j], land(j), True)

    def merge_heads(c):
        def merge(mine, other, last):
            acc, acc_in, mt, mt_in = accs[c], acc_ins[c], mts[c], mt_ins[c]
            for w in range(per_piece):
                m1, t1 = mt[mine, w, 0:1, :], mt[mine, w, 1:2, :]
                m2, t2 = mt_in[other, w, 0:1, :], mt_in[other, w, 1:2, :]
                m = jnp.maximum(m1, m2)
                f1 = jnp.exp2(m1 - m)
                f2 = jnp.exp2(m2 - m)
                t = t1 * f1 + t2 * f2
                rows_w = slice(w * HEAD_SIZE, (w + 1) * HEAD_SIZE)
                a = (
                    acc[mine, rows_w, :].astype(jnp.float32) * f1
                    + acc_in[other, rows_w, :].astype(jnp.float32) * f2
                )
                if last:
                    top = (c % splits * per_piece + w) * HEAD_SIZE
                    col = c // splits * lanes
                    att[top : top + HEAD_SIZE, col : col + lanes] = (a / t).astype(jnp.bfloat16)
                else:
                    mt[mine, w, 0:1, :] = m
                    mt[mine, w, 1:2, :] = t
                    acc[mine, rows_w, :] = a.astype(jnp.bfloat16)

        return merge

    def scatter_of(bufs, inboxes, phase):
        sums = {}

        def adder(c):
            def merge(mine, other, last):
                total = bufs[c][mine].astype(jnp.float32) + inboxes[c][other].astype(jnp.float32)
                if last:
                    sums[c] = total
                else:
                    bufs[c][mine] = total.astype(jnp.bfloat16)

            return merge

        return [Halving(c, [bufs[c]], [inboxes[c]], [phase + c], adder(c)) for c in range(pieces)], sums

    def gather(bufs, phase):
        bases = [place(me, orders[c % 2]) for c in range(pieces)]

        def start(c, j):
            region = bufs[c].at[pl.ds(bases[c], n >> (j + 1))]
            bases[c] = bases[c] - bit[orders[c % 2][j]] * (n >> (j + 1))
            return remote(region, region, phase + c, j, orders[c % 2][j])

        flying = [start(c, bits - 1) for c in range(pieces)]
        for j in reversed(range(bits)):
            for c in range(pieces):
                flying[c].wait_recv()
                if j:
                    flying[c] = start(c, j - 1)

    def join(bufs):
        for i in range(n):
            for c in range(pieces):
                joined[i * tok : (i + 1) * tok, cuts[c] : cuts[c] + bufs[c].shape[2]] = bufs[c][
                    place(i, orders[c % 2])
                ]

    def spread(bufs, c, start, size, val):
        for i in range(n):
            bufs[c][place(i, orders[c % 2]), :, pl.ds(start, size)] = val[i * tok : (i + 1) * tok]

    heads_sum = [
        Halving(c, [mts[c], accs[c]], [mt_ins[c], acc_ins[c]], [2 * splits + c, c], merge_heads(c))
        for c in range(2 * splits)
    ]
    load_wait(("q", 0), ("k", 0), ("v", 0))

    def first_half(g, carry):
        attend(g, 0)
        return carry

    lax.fori_loop(0, STEPS, first_half, 0)
    pl.semaphore_wait(barrier, bits)
    early, late = heads_sum[:splits], heads_sum[splits:]
    for one in early:
        one.start(0)
    load_wait(("q", 1), ("k", 1), ("v", 1))
    for g in range(STEPS):
        attend(g, 1)
        for one in early:
            one.finish(g)
    for one in late:
        one.start(0)
    for j in range(bits):
        for one in (early if j >= STEPS else []) + late:
            one.finish(j)

    load_wait("wo")
    attended = att[...].T
    exchange, sums = scatter_of(parts, part_ins, 4 * splits)
    for c in range(pieces):

        def project(start, size, c=c):
            val = lax.dot_general(
                attended,
                wo[pl.ds(cuts[c] + start, size), :],
                (((1,), (1,)), ((), ())),
                preferred_element_type=jnp.float32,
            ).astype(jnp.bfloat16)
            spread(parts, c, start, size, val)

        chunks(parts[c].shape[2], 256, project)
        exchange[c].start(0)
    for j in range(bits):
        for c in range(pieces):
            exchange[c].finish(j)
    hidden = (
        resid_ref[...].astype(jnp.float32) + jnp.concatenate([sums[c] for c in range(pieces)], axis=1)
    ).astype(jnp.bfloat16)
    normed_here = norm_of(hidden, g1_ref[...].reshape(1, d))
    expert_row = lax.broadcasted_iota(jnp.int32, (EXPERTS, tok), 0)
    picked = jnp.zeros((EXPERTS, tok), jnp.float32)
    for k in range(ids_ref.shape[0]):
        picked += jnp.where(ids_ref[k : k + 1, :] == expert_row, weights_ref[k : k + 1, :], 0.0)
    picked = picked.T
    upper = picked.astype(jnp.bfloat16)
    lower = (picked - upper.astype(jnp.float32)).astype(jnp.bfloat16)
    here = [place(me, orders[c % 2]) for c in range(pieces)]
    final = pieces - 1
    rest = d - cuts[final]
    for c in range(pieces):
        rows1[c][here[c], :, : ends[c] - cuts[c]] = normed_here[:, cuts[c] : ends[c]]
    spot = here[final]
    rows1[final][spot, :, rest:] = jnp.zeros((tok, rows1[final].shape[2] - rest), jnp.bfloat16)
    rows1[final][spot, :, rest : rest + EXPERTS] = upper
    rows1[final][spot, :, rest + EXPERTS : rest + 2 * EXPERTS] = lower
    gather(rows1, 4 * splits + pieces)

    load_wait("gate", "up", "down")
    join(rows1)
    normed = joined[:, :d]
    tags = joined[:, d:].astype(jnp.float32)
    expert = me // (n // EXPERTS)
    lane = lax.broadcasted_iota(jnp.int32, tags.shape, 1)
    weight = jnp.sum(
        jnp.where((lane == expert) | (lane == expert + EXPERTS), tags, 0.0), axis=1, keepdims=True
    )

    def inner(start, size):
        g = lax.dot_general(
            normed,
            gate[pl.ds(start, size), :],
            (((1,), (1,)), ((), ())),
            preferred_element_type=jnp.float32,
        )
        u = lax.dot_general(
            normed,
            up[pl.ds(start, size), :],
            (((1,), (1,)), ((), ())),
            preferred_element_type=jnp.float32,
        )
        act[:, pl.ds(start, size)] = ((u + 1.0) * g * jax.nn.sigmoid(1.702 * g)).astype(
            jnp.bfloat16
        )

    chunks(gate.shape[0], 256, inner)
    active = act[...]
    exchange, sums = scatter_of(parts2, part2_ins, 4 * splits + 2 * pieces)
    for c in range(pieces):

        def outer(start, size, c=c):
            val = (
                jnp.dot(
                    active,
                    down[:, pl.ds(cuts[c] + start, size)],
                    preferred_element_type=jnp.float32,
                )
                * weight
            ).astype(jnp.bfloat16)
            spread(parts2, c, start, size, val)

        chunks(parts2[c].shape[2], 256, outer)
        exchange[c].start(0)
    for j in range(bits):
        for c in range(pieces):
            exchange[c].finish(j)
    stream = (
        hidden.astype(jnp.float32) + jnp.concatenate([sums[c] for c in range(pieces)], axis=1)
    ).astype(jnp.bfloat16)
    stream_ref[...] = stream
    normed_next = norm_of(stream, g2_ref[...].reshape(1, d))
    for c in range(pieces):
        rows2[c][here[c]] = normed_next[:, cuts[c] : ends[c]]
    gather(rows2, 4 * splits + 3 * pieces)
    load_wait("wq")
    join(rows2)
    nq_ref[...] = jnp.dot(
        joined[:, :d], wq[...], preferred_element_type=jnp.float32
    ).astype(jnp.bfloat16)
    for copy in sends:
        copy.wait_send()


def local(
    resid_in,
    queries,
    key_cache,
    value_cache,
    lengths,
    expert_ids,
    expert_weights,
    out_proj,
    gate_proj,
    up_proj,
    down_proj,
    moe_gain,
    attn_gain,
    query_proj,
):
    n = lax.axis_size("seq")
    rows = queries.shape[0]
    tok, d = resid_in.shape
    per_shard = H // n
    bits = n.bit_length() - 1
    order = list(range(bits))
    orders = (tuple(order), tuple([0, 2, 1] + order[3:]))
    full = -(-(d + 2 * EXPERTS) // 128) * 128
    wide = -(-d // (PIECES * 256)) * 256
    cuts = tuple(range(0, d, wide))
    splits = 2 if per_shard % 2 == 0 else 1
    phases = 4 * splits + 4 * len(cuts)
    any_spec = pl.BlockSpec(memory_space=pl.ANY)
    vmem = pl.BlockSpec(memory_space=pltpu.VMEM)
    smem = pl.BlockSpec(memory_space=pltpu.SMEM)
    bf = jnp.bfloat16
    heads = per_shard * HEAD_SIZE
    widths = [b - a for a, b in zip(cuts, cuts[1:] + (d,))]
    tagged = widths[:-1] + [full - cuts[-1]]
    buf = lambda *shape: pltpu.VMEM(shape, bf)
    cols = lambda: tuple(buf(n, tok, w) for w in widths)
    acc = lambda: tuple(buf(n, heads // splits, rows // 2) for _ in range(2 * splits))
    mt_shape = (n, per_shard // splits, 2, rows // 2)
    mt = lambda: tuple(pltpu.VMEM(mt_shape, jnp.float32) for _ in range(2 * splits))
    return pl.pallas_call(
        functools.partial(layer_kernel, n, orders, cuts, splits),
        out_shape=(
            jax.ShapeDtypeStruct((tok, d), bf),
            jax.ShapeDtypeStruct((rows, query_proj.shape[1]), bf),
        ),
        in_specs=[smem] + [any_spec] * 3 + [vmem] * 3 + [any_spec] * 5 + [vmem, vmem],
        out_specs=(vmem, vmem),
        scratch_shapes=[
            buf(*queries.shape),
            buf(*key_cache.shape),
            buf(*value_cache.shape),
            buf(*out_proj.shape[::-1]),
            buf(*gate_proj.shape[::-1]),
            buf(*up_proj.shape[::-1]),
            buf(*down_proj.shape),
            buf(*query_proj.shape),
            acc(),
            mt(),
            acc(),
            mt(),
            cols(),
            cols(),
            cols(),
            cols(),
            tuple(buf(n, tok, w) for w in tagged),
            cols(),
            buf(rows, full),
            buf(rows, gate_proj.shape[1]),
            buf(heads, rows),
            pltpu.VMEM((2, key_cache.shape[1], H // KVH // 2 * QROWS), jnp.float32),
            pltpu.SemaphoreType.DMA((11,)),
            pltpu.SemaphoreType.DMA((phases, bits)),
            pltpu.SemaphoreType.DMA((phases, bits)),
        ],
        compiler_params=pltpu.CompilerParams(
            collective_id=0, has_side_effects=True, vmem_limit_bytes=62 * 2**20
        ),
    )(
        lengths, queries, key_cache, value_cache, resid_in, expert_ids.T, expert_weights.T,
        out_proj.T, gate_proj.T, up_proj.T, down_proj, query_proj, moe_gain, attn_gain,
    )


def solution(mesh):
    placed = (
        P(("group", "seq"), None),
        P("group", None),
        P("group", "seq", None),
        P("group", "seq", None),
        P("group"),
        P(("group", "seq"), None),
        P(("group", "seq"), None),
        P("seq", None),
        P(None, "seq"),
        P(None, "seq"),
        P("seq", None),
        P(),
        P(),
        P(None, "seq"),
    )
    return jax.shard_map(
        local,
        mesh=mesh,
        in_specs=placed,
        out_specs=(P(("group", "seq"), None), P("group", "seq")),
        check_vma=False,
    )
```

```python
import functools
import jax
import jax.numpy as jnp
from jax import lax
from jax.experimental import pallas as pl
from jax.experimental.pallas import tpu as pltpu
from jax.sharding import PartitionSpec as P

H = 64
KVH = 8
HEAD_SIZE = 64
EXPERTS = 16
QROWS = 64
NEG_FILL = -1e30
LOG2E = 1.4426950408889634
PIECES = 6
MESH = pl.DeviceIdType.MESH
STEPS = KVH // 2


def place(i, order):
    out = 0
    for k in order:
        out = out * 2 + (i // 2**k) % 2
    return out


def chunks(total, size, body):
    full = total // size
    if full:

        def step(c, carry):
            body(pl.multiple_of(c * size, size), size)
            return carry

        lax.fori_loop(0, full, step, 0)
    if total % size:
        body(full * size, total % size)


def norm_of(values, gain):
    wide = values.astype(jnp.float32)
    scaled = wide * lax.rsqrt(jnp.mean(wide * wide, axis=-1, keepdims=True) + 1e-05)
    return (scaled * gain).astype(jnp.bfloat16)


def layer_kernel(
    n, orders, cuts, splits,
    len_ref, q_hbm, k_hbm, v_hbm, resid_ref, ids_ref, weights_ref, wo_hbm, gate_hbm, up_hbm,
    down_hbm, wq_hbm, g1_ref, g2_ref,
    stream_ref, nq_ref,
    qb, kb, vb, wo, gate, up, down, wq, accs, mts, acc_ins, mt_ins, parts, part_ins, parts2,
    part2_ins, rows1, rows2, joined, act, att, scores, load_sems, send_sems, recv_sems,
):
    bits = n.bit_length() - 1
    me = lax.axis_index("seq")
    bit = [(me // 2**k) % 2 for k in range(bits)]
    partner = [me + (1 - 2 * bit[k]) * 2**k for k in range(bits)]
    tok, d = resid_ref.shape
    pieces = len(cuts)
    ends = cuts[1:] + (d,)
    per_shard = H // n
    per_piece = per_shard // splits
    requests, span = kb.shape[0], kb.shape[1]
    share = requests // 2
    lanes = share * QROWS
    slots = n // STEPS

    loads = {}

    def load(name, src, dst):
        copy = pltpu.make_async_copy(src, dst, load_sems.at[len(loads)])
        copy.start()
        loads[name] = copy

    for c in range(2):
        rows_c, reqs_c = pl.ds(c * lanes, lanes), pl.ds(c * share, share)
        load(("q", c), q_hbm.at[rows_c], qb.at[rows_c])
        load(("k", c), k_hbm.at[reqs_c], kb.at[reqs_c])
        load(("v", c), v_hbm.at[reqs_c], vb.at[reqs_c])
    load("wo", wo_hbm, wo)
    load("gate", gate_hbm, gate)
    load("up", up_hbm, up)
    load("down", down_hbm, down)
    load("wq", wq_hbm, wq)

    barrier = pltpu.get_barrier_semaphore()
    for k in range(bits):
        pl.semaphore_signal(barrier, inc=1, device_id={"seq": partner[k]}, device_id_type=MESH)

    pairs = H // KVH // 2
    width = pairs * QROWS
    lanes2 = 2 * HEAD_SIZE
    k_lane = lax.broadcasted_iota(jnp.int32, (span, lanes2), 1)
    edge = me * span + lax.broadcasted_iota(jnp.int32, (span, lanes2), 0) - k_lane % QROWS
    q_lane = lax.broadcasted_iota(jnp.int32, (width, lanes2), 1)
    q_row = lax.broadcasted_iota(jnp.int32, (width, lanes2), 0)
    k_low, q_low = k_lane < HEAD_SIZE, q_lane < HEAD_SIZE
    hit = jnp.where(q_lane % QROWS == q_row % QROWS, 1.0, 0.0).astype(jnp.bfloat16)
    ones = jnp.ones((16, span), jnp.bfloat16)
    tile = 128

    def attend(g, c):
        at_g = [place(g * slots, order) for order in orders]
        combos = []
        for r in range(share):
            req = c * share + r
            kv_lanes = pl.ds(pl.multiple_of(g * 128, 128), 128)
            kp = kb[req, :, kv_lanes]
            vt = vb[req, :, kv_lanes].T
            kr = jnp.concatenate([kp[:, HEAD_SIZE:], kp[:, :HEAD_SIZE]], axis=1)
            bar = jnp.where(edge > len_ref[req], NEG_FILL, 0.0).astype(jnp.bfloat16)
            for hh in range(2):
                first = g * 2 * pairs + hh * pairs
                qs = jnp.concatenate(
                    [
                        qb[
                            req * QROWS : (req + 1) * QROWS,
                            pl.ds(pl.multiple_of((first + j) * 128, 128), 128),
                        ]
                        for j in range(pairs)
                    ],
                    axis=0,
                ) * jnp.bfloat16(HEAD_SIZE**-0.5)
                vh = jnp.concatenate([vt[hh * HEAD_SIZE : (hh + 1) * HEAD_SIZE], ones], axis=0)
                for p in range(2):
                    kk = kp if hh == p else kr
                    ka = jnp.where(k_low, bar, kk) if p else jnp.where(k_low, kk, bar)
                    qa = jnp.where(q_low, hit, qs) if p else jnp.where(q_low, qs, hit)
                    combos.append((r, hh, p, ka, qa, vh))

        def score(i):
            ka, qa = combos[i][3:5]
            top = None
            for at in range(0, span, tile):
                s = lax.dot_general(
                    ka[at : at + tile],
                    qa,
                    (((1,), (1,)), ((), ())),
                    preferred_element_type=jnp.float32,
                ) * LOG2E
                scores[i % 2, at : at + tile, :] = s
                here = jnp.max(s.reshape(tile // 8, 8, width), axis=0)
                top = here if top is None else jnp.maximum(top, here)
            return jnp.max(top, axis=0, keepdims=True)

        def weigh(i, m):
            r, hh, p = combos[i][:3]
            vh = combos[i][5]
            base = jnp.maximum(m, NEG_FILL * 0.1)
            acc = None
            for at in range(0, span, tile):
                ch = jnp.exp2((scores[i % 2, at : at + tile, :] - base).astype(jnp.bfloat16))
                one = jnp.dot(vh[:, at : at + tile], ch, preferred_element_type=jnp.float32)
                acc = one if acc is None else acc + one
            t = acc[HEAD_SIZE : HEAD_SIZE + 1]
            acc = acc[:HEAD_SIZE].astype(jnp.bfloat16)
            for j in range(pairs):
                head = hh * (H // KVH) + 2 * j + p
                part, w = divmod(head % per_shard, per_piece)
                part = c * splits + part
                slot = at_g[part % 2] + place(head // per_shard, orders[part % 2])
                src = slice(j * QROWS, (j + 1) * QROWS)
                dst = slice(r * QROWS, (r + 1) * QROWS)
                accs[part][slot, w * HEAD_SIZE : (w + 1) * HEAD_SIZE, dst] = acc[:, src]
                mts[part][slot, w, 0:1, dst] = m[:, src]
                mts[part][slot, w, 1:2, dst] = t[:, src]

        last = None
        for i in range(len(combos) + 1):
            m = score(i) if i < len(combos) else None
            if last is not None:
                weigh(i - 1, last)
            last = m

    def load_wait(*names):
        for name in names:
            loads[name].wait()

    sends = []

    def remote(src, dst, phase, j, k):
        copy = pltpu.make_async_remote_copy(
            src_ref=src,
            dst_ref=dst,
            send_sem=send_sems.at[phase, j],
            recv_sem=recv_sems.at[phase, j],
            device_id={"seq": partner[k]},
            device_id_type=MESH,
        )
        copy.start()
        sends.append(copy)
        return copy

    def land(j):
        return n - 2 * (n >> (j + 1))

    class Halving:
        def __init__(self, c, bufs, inboxes, phases, merge):
            self.order, self.bufs, self.inboxes = orders[c % 2], bufs, inboxes
            self.phases, self.merge, self.flying = phases, merge, {}
            self.keep, self.away, base = [], [], 0
            for j, k in enumerate(self.order):
                half = n >> (j + 1)
                self.away.append(base + (1 - bit[k]) * half)
                base = base + bit[k] * half
                self.keep.append(base)

        def start(self, j):
            half = n >> (j + 1)
            self.flying[j] = [
                remote(
                    buf.at[pl.ds(self.away[j], half)],
                    inbox.at[pl.ds(land(j), half)],
                    phase,
                    j,
                    self.order[j],
                )
                for buf, inbox, phase in zip(self.bufs, self.inboxes, self.phases)
            ]

        def finish(self, j):
            for copy in self.flying[j]:
                copy.wait_recv()
            if j < bits - 1:

                def step(x, carry):
                    self.merge(self.keep[j] + x, land(j) + x, False)
                    return carry

                lax.fori_loop(0, n >> (j + 1), step, 0)
                self.start(j + 1)
            else:
                self.merge(self.keep[j], land(j), True)

    def merge_heads(c):
        def merge(mine, other, last):
            acc, acc_in, mt, mt_in = accs[c], acc_ins[c], mts[c], mt_ins[c]
            for w in range(per_piece):
                m1, t1 = mt[mine, w, 0:1, :], mt[mine, w, 1:2, :]
                m2, t2 = mt_in[other, w, 0:1, :], mt_in[other, w, 1:2, :]
                m = jnp.maximum(m1, m2)
                f1 = jnp.exp2(m1 - m)
                f2 = jnp.exp2(m2 - m)
                t = t1 * f1 + t2 * f2
                rows_w = slice(w * HEAD_SIZE, (w + 1) * HEAD_SIZE)
                a = (
                    acc[mine, rows_w, :].astype(jnp.float32) * f1
                    + acc_in[other, rows_w, :].astype(jnp.float32) * f2
                )
                if last:
                    top = (c % splits * per_piece + w) * HEAD_SIZE
                    col = c // splits * lanes
                    att[top : top + HEAD_SIZE, col : col + lanes] = (a / t).astype(jnp.bfloat16)
                else:
                    mt[mine, w, 0:1, :] = m
                    mt[mine, w, 1:2, :] = t
                    acc[mine, rows_w, :] = a.astype(jnp.bfloat16)

        return merge

    def scatter_of(bufs, inboxes, phase):
        sums = {}

        def adder(c):
            def merge(mine, other, last):
                total = bufs[c][mine].astype(jnp.float32) + inboxes[c][other].astype(jnp.float32)
                if last:
                    sums[c] = total
                else:
                    bufs[c][mine] = total.astype(jnp.bfloat16)

            return merge

        return [Halving(c, [bufs[c]], [inboxes[c]], [phase + c], adder(c)) for c in range(pieces)], sums

    def gather(bufs, phase):
        bases = [place(me, orders[c % 2]) for c in range(pieces)]

        def start(c, j):
            region = bufs[c].at[pl.ds(bases[c], n >> (j + 1))]
            bases[c] = bases[c] - bit[orders[c % 2][j]] * (n >> (j + 1))
            return remote(region, region, phase + c, j, orders[c % 2][j])

        flying = [start(c, bits - 1) for c in range(pieces)]
        for j in reversed(range(bits)):
            for c in range(pieces):
                flying[c].wait_recv()
                if j:
                    flying[c] = start(c, j - 1)

    def join(bufs):
        for i in range(n):
            for c in range(pieces):
                joined[i * tok : (i + 1) * tok, cuts[c] : cuts[c] + bufs[c].shape[2]] = bufs[c][
                    place(i, orders[c % 2])
                ]

    def spread(bufs, c, start, size, val):
        for i in range(n):
            bufs[c][place(i, orders[c % 2]), :, pl.ds(start, size)] = val[i * tok : (i + 1) * tok]

    heads_sum = [
        Halving(c, [mts[c], accs[c]], [mt_ins[c], acc_ins[c]], [2 * splits + c, c], merge_heads(c))
        for c in range(2 * splits)
    ]
    load_wait(("q", 0), ("k", 0), ("v", 0))

    def first_half(g, carry):
        attend(g, 0)
        return carry

    lax.fori_loop(0, STEPS, first_half, 0)
    pl.semaphore_wait(barrier, bits)
    early, late = heads_sum[:splits], heads_sum[splits:]
    for one in early:
        one.start(0)
    load_wait(("q", 1), ("k", 1), ("v", 1))
    for g in range(STEPS):
        attend(g, 1)
        for one in early:
            one.finish(g)
    for one in late:
        one.start(0)
    for j in range(bits):
        for one in (early if j >= STEPS else []) + late:
            one.finish(j)

    load_wait("wo")
    attended = att[...].T
    exchange, sums = scatter_of(parts, part_ins, 4 * splits)
    for c in range(pieces):

        def project(start, size, c=c):
            val = lax.dot_general(
                attended,
                wo[pl.ds(cuts[c] + start, size), :],
                (((1,), (1,)), ((), ())),
                preferred_element_type=jnp.float32,
            ).astype(jnp.bfloat16)
            spread(parts, c, start, size, val)

        chunks(parts[c].shape[2], 256, project)
        exchange[c].start(0)
        if c:
            exchange[c - 1].finish(0)
    exchange[pieces - 1].finish(0)
    for j in range(1, bits):
        for c in range(pieces):
            exchange[c].finish(j)
    hidden = (
        resid_ref[...].astype(jnp.float32) + jnp.concatenate([sums[c] for c in range(pieces)], axis=1)
    ).astype(jnp.bfloat16)
    normed_here = norm_of(hidden, g1_ref[...].reshape(1, d))
    expert_row = lax.broadcasted_iota(jnp.int32, (EXPERTS, tok), 0)
    picked = jnp.zeros((EXPERTS, tok), jnp.float32)
    for k in range(ids_ref.shape[0]):
        picked += jnp.where(ids_ref[k : k + 1, :] == expert_row, weights_ref[k : k + 1, :], 0.0)
    picked = picked.T
    upper = picked.astype(jnp.bfloat16)
    lower = (picked - upper.astype(jnp.float32)).astype(jnp.bfloat16)
    here = [place(me, orders[c % 2]) for c in range(pieces)]
    final = pieces - 1
    rest = d - cuts[final]
    for c in range(pieces):
        rows1[c][here[c], :, : ends[c] - cuts[c]] = normed_here[:, cuts[c] : ends[c]]
    spot = here[final]
    rows1[final][spot, :, rest:] = jnp.zeros((tok, rows1[final].shape[2] - rest), jnp.bfloat16)
    rows1[final][spot, :, rest : rest + EXPERTS] = upper
    rows1[final][spot, :, rest + EXPERTS : rest + 2 * EXPERTS] = lower
    gather(rows1, 4 * splits + pieces)

    load_wait("gate", "up", "down")
    join(rows1)
    normed = joined[:, :d]
    tags = joined[:, d:].astype(jnp.float32)
    expert = me // (n // EXPERTS)
    lane = lax.broadcasted_iota(jnp.int32, tags.shape, 1)
    weight = jnp.sum(
        jnp.where((lane == expert) | (lane == expert + EXPERTS), tags, 0.0), axis=1, keepdims=True
    )

    def inner(start, size):
        g = lax.dot_general(
            normed,
            gate[pl.ds(start, size), :],
            (((1,), (1,)), ((), ())),
            preferred_element_type=jnp.float32,
        )
        u = lax.dot_general(
            normed,
            up[pl.ds(start, size), :],
            (((1,), (1,)), ((), ())),
            preferred_element_type=jnp.float32,
        )
        act[:, pl.ds(start, size)] = ((u + 1.0) * g * jax.nn.sigmoid(1.702 * g)).astype(
            jnp.bfloat16
        )

    chunks(gate.shape[0], 256, inner)
    active = act[...]
    exchange, sums = scatter_of(parts2, part2_ins, 4 * splits + 2 * pieces)
    for c in range(pieces):

        def outer(start, size, c=c):
            val = (
                jnp.dot(
                    active,
                    down[:, pl.ds(cuts[c] + start, size)],
                    preferred_element_type=jnp.float32,
                )
                * weight
            ).astype(jnp.bfloat16)
            spread(parts2, c, start, size, val)

        chunks(parts2[c].shape[2], 256, outer)
        exchange[c].start(0)
        if c:
            exchange[c - 1].finish(0)
    exchange[pieces - 1].finish(0)
    for j in range(1, bits):
        for c in range(pieces):
            exchange[c].finish(j)
    stream = (
        hidden.astype(jnp.float32) + jnp.concatenate([sums[c] for c in range(pieces)], axis=1)
    ).astype(jnp.bfloat16)
    stream_ref[...] = stream
    normed_next = norm_of(stream, g2_ref[...].reshape(1, d))
    for c in range(pieces):
        rows2[c][here[c]] = normed_next[:, cuts[c] : ends[c]]
    gather(rows2, 4 * splits + 3 * pieces)
    load_wait("wq")
    join(rows2)
    nq_ref[...] = jnp.dot(
        joined[:, :d], wq[...], preferred_element_type=jnp.float32
    ).astype(jnp.bfloat16)
    for copy in sends:
        copy.wait_send()


def hand_over(stream_in, nq_in, stream_ref, nq_ref):
    stream_ref[...] = stream_in[...]
    nq_ref[...] = nq_in[...]


def local(
    resid_in,
    queries,
    key_cache,
    value_cache,
    lengths,
    expert_ids,
    expert_weights,
    out_proj,
    gate_proj,
    up_proj,
    down_proj,
    moe_gain,
    attn_gain,
    query_proj,
):
    n = lax.axis_size("seq")
    rows = queries.shape[0]
    tok, d = resid_in.shape
    per_shard = H // n
    bits = n.bit_length() - 1
    order = list(range(bits))
    orders = (tuple(order), tuple([0, 2, 1] + order[3:]))
    full = -(-(d + 2 * EXPERTS) // 128) * 128
    wide = -(-d // (PIECES * 256)) * 256
    cuts = tuple(range(0, d, wide))
    splits = 2 if per_shard % 2 == 0 else 1
    phases = 4 * splits + 4 * len(cuts)
    any_spec = pl.BlockSpec(memory_space=pl.ANY)
    vmem = pl.BlockSpec(memory_space=pltpu.VMEM)
    smem = pl.BlockSpec(memory_space=pltpu.SMEM)
    bf = jnp.bfloat16
    heads = per_shard * HEAD_SIZE
    widths = [b - a for a, b in zip(cuts, cuts[1:] + (d,))]
    tagged = widths[:-1] + [full - cuts[-1]]
    buf = lambda *shape: pltpu.VMEM(shape, bf)
    cols = lambda: tuple(buf(n, tok, w) for w in widths)
    acc = lambda: tuple(buf(n, heads // splits, rows // 2) for _ in range(2 * splits))
    mt_shape = (n, per_shard // splits, 2, rows // 2)
    mt = lambda: tuple(pltpu.VMEM(mt_shape, jnp.float32) for _ in range(2 * splits))
    stream, nq = pl.pallas_call(
        functools.partial(layer_kernel, n, orders, cuts, splits),
        out_shape=(
            jax.ShapeDtypeStruct((tok, d), bf),
            jax.ShapeDtypeStruct((rows, query_proj.shape[1]), bf),
        ),
        in_specs=[smem] + [any_spec] * 3 + [vmem] * 3 + [any_spec] * 5 + [vmem, vmem],
        out_specs=(vmem, vmem),
        scratch_shapes=[
            buf(*queries.shape),
            buf(*key_cache.shape),
            buf(*value_cache.shape),
            buf(*out_proj.shape[::-1]),
            buf(*gate_proj.shape[::-1]),
            buf(*up_proj.shape[::-1]),
            buf(*down_proj.shape),
            buf(*query_proj.shape),
            acc(),
            mt(),
            acc(),
            mt(),
            cols(),
            cols(),
            cols(),
            cols(),
            tuple(buf(n, tok, w) for w in tagged),
            cols(),
            buf(rows, full),
            buf(rows, gate_proj.shape[1]),
            buf(heads, rows),
            pltpu.VMEM((2, key_cache.shape[1], H // KVH // 2 * QROWS), jnp.float32),
            pltpu.SemaphoreType.DMA((11,)),
            pltpu.SemaphoreType.DMA((phases, bits)),
            pltpu.SemaphoreType.DMA((phases, bits)),
        ],
        compiler_params=pltpu.CompilerParams(
            collective_id=0, has_side_effects=True, vmem_limit_bytes=62 * 2**20
        ),
    )(
        lengths, queries, key_cache, value_cache, resid_in, expert_ids.T, expert_weights.T,
        out_proj.T, gate_proj.T, up_proj.T, down_proj, query_proj, moe_gain, attn_gain,
    )
    return pl.pallas_call(
        hand_over,
        out_shape=(
            jax.ShapeDtypeStruct(stream.shape, bf),
            jax.ShapeDtypeStruct(nq.shape, bf),
        ),
        in_specs=[vmem, vmem],
        out_specs=(vmem, vmem),
    )(stream, nq)


def solution(mesh):
    placed = (
        P(("group", "seq"), None),
        P("group", None),
        P("group", "seq", None),
        P("group", "seq", None),
        P("group"),
        P(("group", "seq"), None),
        P(("group", "seq"), None),
        P("seq", None),
        P(None, "seq"),
        P(None, "seq"),
        P("seq", None),
        P(),
        P(),
        P(None, "seq"),
    )
    return jax.shard_map(
        local,
        mesh=mesh,
        in_specs=placed,
        out_specs=(P(("group", "seq"), None), P("group", "seq")),
        check_vma=False,
    )
```

```python
import functools
import jax
import jax.numpy as jnp
from jax import lax
from jax.experimental import pallas as pl
from jax.experimental.pallas import tpu as pltpu
from jax.sharding import PartitionSpec as P

H = 64
KVH = 8
HEAD_SIZE = 64
EXPERTS = 16
QROWS = 64
NEG_FILL = -1e30
LOG2E = 1.4426950408889634
PIECES = 6
MESH = pl.DeviceIdType.MESH
STEPS = KVH // 2


def place(i, order):
    out = 0
    for k in order:
        out = out * 2 + (i // 2**k) % 2
    return out


def chunks(total, size, body):
    full = total // size
    if full:

        def step(c, carry):
            body(pl.multiple_of(c * size, size), size)
            return carry

        lax.fori_loop(0, full, step, 0)
    if total % size:
        body(full * size, total % size)


def norm_of(values, gain):
    wide = values.astype(jnp.float32)
    scaled = wide * lax.rsqrt(jnp.mean(wide * wide, axis=-1, keepdims=True) + 1e-05)
    return (scaled * gain).astype(jnp.bfloat16)


def layer_kernel(
    n, orders, cuts, splits,
    len_ref, q_hbm, k_hbm, v_hbm, resid_ref, ids_ref, weights_ref, wo_hbm, gate_hbm, up_hbm,
    down_hbm, wq_hbm, g1_ref, g2_ref,
    stream_ref, nq_ref,
    qb, kb, vb, wo, gate, up, down, wq, accs, mts, acc_ins, mt_ins, parts, part_ins, parts2,
    part2_ins, rows1, rows2, joined, act, att, scores, load_sems, send_sems, recv_sems,
):
    bits = n.bit_length() - 1
    me = lax.axis_index("seq")
    bit = [(me // 2**k) % 2 for k in range(bits)]
    partner = [me + (1 - 2 * bit[k]) * 2**k for k in range(bits)]
    tok, d = resid_ref.shape
    pieces = len(cuts)
    ends = cuts[1:] + (d,)
    per_shard = H // n
    per_piece = per_shard // splits
    requests, span = kb.shape[0], kb.shape[1]
    share = requests // 2
    lanes = share * QROWS
    slots = n // STEPS

    loads = {}

    def load(name, src, dst):
        copy = pltpu.make_async_copy(src, dst, load_sems.at[len(loads)])
        copy.start()
        loads[name] = copy

    for c in range(2):
        rows_c, reqs_c = pl.ds(c * lanes, lanes), pl.ds(c * share, share)
        load(("q", c), q_hbm.at[rows_c], qb.at[rows_c])
        load(("k", c), k_hbm.at[reqs_c], kb.at[reqs_c])
        load(("v", c), v_hbm.at[reqs_c], vb.at[reqs_c])
    load("wo", wo_hbm, wo)
    load("gate", gate_hbm, gate)
    load("up", up_hbm, up)
    load("down", down_hbm, down)
    load("wq", wq_hbm, wq)

    barrier = pltpu.get_barrier_semaphore()
    for k in range(bits):
        pl.semaphore_signal(barrier, inc=1, device_id={"seq": partner[k]}, device_id_type=MESH)

    pairs = H // KVH // 2
    width = pairs * QROWS
    lanes2 = 2 * HEAD_SIZE
    k_lane = lax.broadcasted_iota(jnp.int32, (span, lanes2), 1)
    edge = me * span + lax.broadcasted_iota(jnp.int32, (span, lanes2), 0) - k_lane % QROWS
    q_lane = lax.broadcasted_iota(jnp.int32, (width, lanes2), 1)
    q_row = lax.broadcasted_iota(jnp.int32, (width, lanes2), 0)
    k_low, q_low = k_lane < HEAD_SIZE, q_lane < HEAD_SIZE
    hit = jnp.where(q_lane % QROWS == q_row % QROWS, 1.0, 0.0).astype(jnp.bfloat16)
    ones = jnp.ones((16, span), jnp.bfloat16)
    tile = 128

    def attend(g, c):
        at_g = [place(g * slots, order) for order in orders]
        combos = []
        for r in range(share):
            req = c * share + r
            kv_lanes = pl.ds(pl.multiple_of(g * 128, 128), 128)
            kp = kb[req, :, kv_lanes]
            vt = vb[req, :, kv_lanes].T
            kr = jnp.concatenate([kp[:, HEAD_SIZE:], kp[:, :HEAD_SIZE]], axis=1)
            bar = jnp.where(edge > len_ref[req], NEG_FILL, 0.0).astype(jnp.bfloat16)
            for hh in range(2):
                first = g * 2 * pairs + hh * pairs
                qs = jnp.concatenate(
                    [
                        qb[
                            req * QROWS : (req + 1) * QROWS,
                            pl.ds(pl.multiple_of((first + j) * 128, 128), 128),
                        ]
                        for j in range(pairs)
                    ],
                    axis=0,
                ) * jnp.bfloat16(HEAD_SIZE**-0.5)
                vh = jnp.concatenate([vt[hh * HEAD_SIZE : (hh + 1) * HEAD_SIZE], ones], axis=0)
                for p in range(2):
                    kk = kp if hh == p else kr
                    ka = jnp.where(k_low, bar, kk) if p else jnp.where(k_low, kk, bar)
                    qa = jnp.where(q_low, hit, qs) if p else jnp.where(q_low, qs, hit)
                    combos.append((r, hh, p, ka, qa, vh))

        def score(i):
            ka, qa = combos[i][3:5]
            top = None
            for at in range(0, span, tile):
                s = lax.dot_general(
                    ka[at : at + tile],
                    qa,
                    (((1,), (1,)), ((), ())),
                    preferred_element_type=jnp.float32,
                ) * LOG2E
                scores[i % 2, at : at + tile, :] = s
                here = jnp.max(s.reshape(tile // 8, 8, width), axis=0)
                top = here if top is None else jnp.maximum(top, here)
            return jnp.max(top, axis=0, keepdims=True)

        def weigh(i, m):
            r, hh, p = combos[i][:3]
            vh = combos[i][5]
            base = jnp.maximum(m, NEG_FILL * 0.1)
            acc = None
            for at in range(0, span, tile):
                ch = jnp.exp2((scores[i % 2, at : at + tile, :] - base).astype(jnp.bfloat16))
                one = jnp.dot(vh[:, at : at + tile], ch, preferred_element_type=jnp.float32)
                acc = one if acc is None else acc + one
            t = acc[HEAD_SIZE : HEAD_SIZE + 1]
            acc = acc[:HEAD_SIZE].astype(jnp.bfloat16)
            for j in range(pairs):
                head = hh * (H // KVH) + 2 * j + p
                part, w = divmod(head % per_shard, per_piece)
                part = c * splits + part
                slot = at_g[part % 2] + place(head // per_shard, orders[part % 2])
                src = slice(j * QROWS, (j + 1) * QROWS)
                dst = slice(r * QROWS, (r + 1) * QROWS)
                accs[part][slot, w * HEAD_SIZE : (w + 1) * HEAD_SIZE, dst] = acc[:, src]
                mts[part][slot, w, 0:1, dst] = m[:, src]
                mts[part][slot, w, 1:2, dst] = t[:, src]

        last = None
        for i in range(len(combos) + 1):
            m = score(i) if i < len(combos) else None
            if last is not None:
                weigh(i - 1, last)
            last = m

    def load_wait(*names):
        for name in names:
            loads[name].wait()

    sends = []

    def remote(src, dst, phase, j, k):
        copy = pltpu.make_async_remote_copy(
            src_ref=src,
            dst_ref=dst,
            send_sem=send_sems.at[phase, j],
            recv_sem=recv_sems.at[phase, j],
            device_id={"seq": partner[k]},
            device_id_type=MESH,
        )
        copy.start()
        sends.append(copy)
        return copy

    def land(j):
        return n - 2 * (n >> (j + 1))

    class Halving:
        def __init__(self, c, bufs, inboxes, phases, merge):
            self.order, self.bufs, self.inboxes = orders[c % 2], bufs, inboxes
            self.phases, self.merge, self.flying = phases, merge, {}
            self.keep, self.away, base = [], [], 0
            for j, k in enumerate(self.order):
                half = n >> (j + 1)
                self.away.append(base + (1 - bit[k]) * half)
                base = base + bit[k] * half
                self.keep.append(base)

        def start(self, j):
            half = n >> (j + 1)
            self.flying[j] = [
                remote(
                    buf.at[pl.ds(self.away[j], half)],
                    inbox.at[pl.ds(land(j), half)],
                    phase,
                    j,
                    self.order[j],
                )
                for buf, inbox, phase in zip(self.bufs, self.inboxes, self.phases)
            ]

        def finish(self, j):
            for copy in self.flying[j]:
                copy.wait_recv()
            if j < bits - 1:

                def step(x, carry):
                    self.merge(self.keep[j] + x, land(j) + x, False)
                    return carry

                lax.fori_loop(0, n >> (j + 1), step, 0)
                self.start(j + 1)
            else:
                self.merge(self.keep[j], land(j), True)

    def merge_heads(c):
        def merge(mine, other, last):
            acc, acc_in, mt, mt_in = accs[c], acc_ins[c], mts[c], mt_ins[c]
            for w in range(per_piece):
                m1, t1 = mt[mine, w, 0:1, :], mt[mine, w, 1:2, :]
                m2, t2 = mt_in[other, w, 0:1, :], mt_in[other, w, 1:2, :]
                m = jnp.maximum(m1, m2)
                f1 = jnp.exp2(m1 - m)
                f2 = jnp.exp2(m2 - m)
                t = t1 * f1 + t2 * f2
                rows_w = slice(w * HEAD_SIZE, (w + 1) * HEAD_SIZE)
                a = (
                    acc[mine, rows_w, :].astype(jnp.float32) * f1
                    + acc_in[other, rows_w, :].astype(jnp.float32) * f2
                )
                if last:
                    top = (c % splits * per_piece + w) * HEAD_SIZE
                    col = c // splits * lanes
                    att[top : top + HEAD_SIZE, col : col + lanes] = (a / t).astype(jnp.bfloat16)
                else:
                    mt[mine, w, 0:1, :] = m
                    mt[mine, w, 1:2, :] = t
                    acc[mine, rows_w, :] = a.astype(jnp.bfloat16)

        return merge

    def scatter_of(bufs, inboxes, phase):
        sums = {}

        def adder(c):
            def merge(mine, other, last):
                total = bufs[c][mine].astype(jnp.float32) + inboxes[c][other].astype(jnp.float32)
                if last:
                    sums[c] = total
                else:
                    bufs[c][mine] = total.astype(jnp.bfloat16)

            return merge

        return [Halving(c, [bufs[c]], [inboxes[c]], [phase + c], adder(c)) for c in range(pieces)], sums

    def join(bufs, c):
        for i in range(n):
            joined[i * tok : (i + 1) * tok, cuts[c] : cuts[c] + bufs[c].shape[2]] = bufs[c][
                place(i, orders[c % 2])
            ]

    def gather(bufs, phase):
        bases = [place(me, orders[c % 2]) for c in range(pieces)]

        def start(c, j):
            region = bufs[c].at[pl.ds(bases[c], n >> (j + 1))]
            bases[c] = bases[c] - bit[orders[c % 2][j]] * (n >> (j + 1))
            return remote(region, region, phase + c, j, orders[c % 2][j])

        flying = [start(c, bits - 1) for c in range(pieces)]
        for j in reversed(range(bits)):
            for c in range(pieces):
                flying[c].wait_recv()
                if j:
                    flying[c] = start(c, j - 1)
                else:
                    join(bufs, c)

    def spread(bufs, c, start, size, val):
        for i in range(n):
            bufs[c][place(i, orders[c % 2]), :, pl.ds(start, size)] = val[i * tok : (i + 1) * tok]

    heads_sum = [
        Halving(c, [mts[c], accs[c]], [mt_ins[c], acc_ins[c]], [2 * splits + c, c], merge_heads(c))
        for c in range(2 * splits)
    ]
    load_wait(("q", 0), ("k", 0), ("v", 0))

    def first_half(g, carry):
        attend(g, 0)
        return carry

    lax.fori_loop(0, STEPS, first_half, 0)
    pl.semaphore_wait(barrier, bits)
    early, late = heads_sum[:splits], heads_sum[splits:]
    for one in early:
        one.start(0)
    load_wait(("q", 1), ("k", 1), ("v", 1))
    for g in range(STEPS):
        attend(g, 1)
        for one in early:
            one.finish(g)
    for one in late:
        one.start(0)
    for j in range(bits):
        for one in (early if j >= STEPS else []) + late:
            one.finish(j)

    load_wait("wo")
    attended = att[...].T
    exchange, sums = scatter_of(parts, part_ins, 4 * splits)
    for c in range(pieces):

        def project(start, size, c=c):
            val = lax.dot_general(
                attended,
                wo[pl.ds(cuts[c] + start, size), :],
                (((1,), (1,)), ((), ())),
                preferred_element_type=jnp.float32,
            ).astype(jnp.bfloat16)
            spread(parts, c, start, size, val)

        chunks(parts[c].shape[2], 512, project)
        exchange[c].start(0)
        if c:
            exchange[c - 1].finish(0)
    exchange[pieces - 1].finish(0)
    for j in range(1, bits):
        for c in range(pieces):
            exchange[c].finish(j)
    hidden = (
        resid_ref[...].astype(jnp.float32) + jnp.concatenate([sums[c] for c in range(pieces)], axis=1)
    ).astype(jnp.bfloat16)
    normed_here = norm_of(hidden, g1_ref[...].reshape(1, d))
    expert_row = lax.broadcasted_iota(jnp.int32, (EXPERTS, tok), 0)
    picked = jnp.zeros((EXPERTS, tok), jnp.float32)
    for k in range(ids_ref.shape[0]):
        picked += jnp.where(ids_ref[k : k + 1, :] == expert_row, weights_ref[k : k + 1, :], 0.0)
    picked = picked.T
    upper = picked.astype(jnp.bfloat16)
    lower = (picked - upper.astype(jnp.float32)).astype(jnp.bfloat16)
    here = [place(me, orders[c % 2]) for c in range(pieces)]
    final = pieces - 1
    rest = d - cuts[final]
    for c in range(pieces):
        rows1[c][here[c], :, : ends[c] - cuts[c]] = normed_here[:, cuts[c] : ends[c]]
    spot = here[final]
    rows1[final][spot, :, rest:] = jnp.zeros((tok, rows1[final].shape[2] - rest), jnp.bfloat16)
    rows1[final][spot, :, rest : rest + EXPERTS] = upper
    rows1[final][spot, :, rest + EXPERTS : rest + 2 * EXPERTS] = lower
    gather(rows1, 4 * splits + pieces)

    load_wait("gate", "up", "down")
    normed = joined[:, :d]
    tags = joined[:, d:].astype(jnp.float32)
    expert = me // (n // EXPERTS)
    lane = lax.broadcasted_iota(jnp.int32, tags.shape, 1)
    weight = jnp.sum(
        jnp.where((lane == expert) | (lane == expert + EXPERTS), tags, 0.0), axis=1, keepdims=True
    )

    def inner(start, size):
        g = lax.dot_general(
            normed,
            gate[pl.ds(start, size), :],
            (((1,), (1,)), ((), ())),
            preferred_element_type=jnp.float32,
        )
        u = lax.dot_general(
            normed,
            up[pl.ds(start, size), :],
            (((1,), (1,)), ((), ())),
            preferred_element_type=jnp.float32,
        )
        act[:, pl.ds(start, size)] = ((u + 1.0) * g * jax.nn.sigmoid(1.702 * g)).astype(
            jnp.bfloat16
        )

    chunks(gate.shape[0], 256, inner)
    active = act[...]
    exchange, sums = scatter_of(parts2, part2_ins, 4 * splits + 2 * pieces)
    for c in range(pieces):

        def outer(start, size, c=c):
            val = (
                jnp.dot(
                    active,
                    down[:, pl.ds(cuts[c] + start, size)],
                    preferred_element_type=jnp.float32,
                )
                * weight
            ).astype(jnp.bfloat16)
            spread(parts2, c, start, size, val)

        chunks(parts2[c].shape[2], 512, outer)
        exchange[c].start(0)
        if c:
            exchange[c - 1].finish(0)
    exchange[pieces - 1].finish(0)
    for j in range(1, bits):
        for c in range(pieces):
            exchange[c].finish(j)
    stream = (
        hidden.astype(jnp.float32) + jnp.concatenate([sums[c] for c in range(pieces)], axis=1)
    ).astype(jnp.bfloat16)
    stream_ref[...] = stream
    normed_next = norm_of(stream, g2_ref[...].reshape(1, d))
    for c in range(pieces):
        rows2[c][here[c]] = normed_next[:, cuts[c] : ends[c]]
    gather(rows2, 4 * splits + 3 * pieces)
    load_wait("wq")
    nq_ref[...] = jnp.dot(
        joined[:, :d], wq[...], preferred_element_type=jnp.float32
    ).astype(jnp.bfloat16)
    for copy in sends:
        copy.wait_send()


def hand_over(stream_in, nq_in, stream_ref, nq_ref):
    stream_ref[...] = stream_in[...]
    nq_ref[...] = nq_in[...]


def local(
    resid_in,
    queries,
    key_cache,
    value_cache,
    lengths,
    expert_ids,
    expert_weights,
    out_proj,
    gate_proj,
    up_proj,
    down_proj,
    moe_gain,
    attn_gain,
    query_proj,
):
    n = lax.axis_size("seq")
    rows = queries.shape[0]
    tok, d = resid_in.shape
    per_shard = H // n
    bits = n.bit_length() - 1
    order = list(range(bits))
    orders = (tuple(order), tuple([0, 2, 1] + order[3:]))
    full = -(-(d + 2 * EXPERTS) // 128) * 128
    wide = -(-d // (PIECES * 256)) * 256
    cuts = tuple(range(0, d, wide))
    splits = 2 if per_shard % 2 == 0 else 1
    phases = 4 * splits + 4 * len(cuts)
    any_spec = pl.BlockSpec(memory_space=pl.ANY)
    vmem = pl.BlockSpec(memory_space=pltpu.VMEM)
    smem = pl.BlockSpec(memory_space=pltpu.SMEM)
    bf = jnp.bfloat16
    heads = per_shard * HEAD_SIZE
    widths = [b - a for a, b in zip(cuts, cuts[1:] + (d,))]
    tagged = widths[:-1] + [full - cuts[-1]]
    buf = lambda *shape: pltpu.VMEM(shape, bf)
    cols = lambda: tuple(buf(n, tok, w) for w in widths)
    acc = lambda: tuple(buf(n, heads // splits, rows // 2) for _ in range(2 * splits))
    mt_shape = (n, per_shard // splits, 2, rows // 2)
    mt = lambda: tuple(pltpu.VMEM(mt_shape, jnp.float32) for _ in range(2 * splits))
    stream, nq = pl.pallas_call(
        functools.partial(layer_kernel, n, orders, cuts, splits),
        out_shape=(
            jax.ShapeDtypeStruct((tok, d), bf),
            jax.ShapeDtypeStruct((rows, query_proj.shape[1]), bf),
        ),
        in_specs=[smem] + [any_spec] * 3 + [vmem] * 3 + [any_spec] * 5 + [vmem, vmem],
        out_specs=(vmem, vmem),
        scratch_shapes=[
            buf(*queries.shape),
            buf(*key_cache.shape),
            buf(*value_cache.shape),
            buf(*out_proj.shape[::-1]),
            buf(*gate_proj.shape[::-1]),
            buf(*up_proj.shape[::-1]),
            buf(*down_proj.shape),
            buf(*query_proj.shape),
            acc(),
            mt(),
            acc(),
            mt(),
            cols(),
            cols(),
            cols(),
            cols(),
            tuple(buf(n, tok, w) for w in tagged),
            cols(),
            buf(rows, full),
            buf(rows, gate_proj.shape[1]),
            buf(heads, rows),
            pltpu.VMEM((2, key_cache.shape[1], H // KVH // 2 * QROWS), jnp.float32),
            pltpu.SemaphoreType.DMA((11,)),
            pltpu.SemaphoreType.DMA((phases, bits)),
            pltpu.SemaphoreType.DMA((phases, bits)),
        ],
        compiler_params=pltpu.CompilerParams(
            collective_id=0, has_side_effects=True, vmem_limit_bytes=62 * 2**20
        ),
    )(
        lengths, queries, key_cache, value_cache, resid_in, expert_ids.T, expert_weights.T,
        out_proj.T, gate_proj.T, up_proj.T, down_proj, query_proj, moe_gain, attn_gain,
    )
    return pl.pallas_call(
        hand_over,
        out_shape=(
            jax.ShapeDtypeStruct(stream.shape, bf),
            jax.ShapeDtypeStruct(nq.shape, bf),
        ),
        in_specs=[vmem, vmem],
        out_specs=(vmem, vmem),
    )(stream, nq)


def solution(mesh):
    placed = (
        P(("group", "seq"), None),
        P("group", None),
        P("group", "seq", None),
        P("group", "seq", None),
        P("group"),
        P(("group", "seq"), None),
        P(("group", "seq"), None),
        P("seq", None),
        P(None, "seq"),
        P(None, "seq"),
        P("seq", None),
        P(),
        P(),
        P(None, "seq"),
    )
    return jax.shard_map(
        local,
        mesh=mesh,
        in_specs=placed,
        out_specs=(P(("group", "seq"), None), P("group", "seq")),
        check_vma=False,
    )
```
